32 devices in a mesh: dp: 4 (over y, x), expert: 8 (over z, core).
Axes of the slice: x: 2, y: 2, z: 4, core: 2. Of those that a mesh axis runs over, the one named last changes fastest.
Arguments:
- tokens: bfloat16 [5120, 1024], P(('dp', 'expert')), may hold values from -6 to 6
- expert_ids: int32 [5120, 2], P(('dp', 'expert')), may hold values from 0 to 15, all different within a row; in each aligned block of 160 rows (0 to 159, 160 to 319, ...) at most 40 rows name the same one
- router: bfloat16 [1024, 16], replicated, may hold values from -0.5 to 0.5
- gate_up_weight: bfloat16 [16, 1024, 2048], P('expert', 'dp'), may hold values from -0.1875 to 0.1875
- down_weight: bfloat16 [16, 1024, 1024], P('expert', 'dp'), may hold values from -0.1875 to 0.1875
- out_grad: bfloat16 [5120, 1024], P(('dp', 'expert')), may hold values from -6 to 6
Outputs:
- mixed_out: bfloat16 [5120, 1024], P(('dp', 'expert'))
- tokens_grad: bfloat16 [5120, 1024], P(('dp', 'expert'))
- router_grad: float32 [1024, 16], replicated
- gate_up_grad: float32 [16, 1024, 2048], P('expert', 'dp')
- down_grad: float32 [16, 1024, 1024], P('expert', 'dp')
The draws below stay inside these ranges and needn't reach their ends.
Inputs may be any that keep to these rules, and one draw needn't show every extreme that they name: `expert_ids`: the 2 experts of a token differ. Among the 160 tokens of one device no expert is named more than 40 times, and in every draw some expert is named exactly 40 times by the tokens of some device.
All inputs are finite; a program needn't handle non-finite values.
Results may differ from the reference program's by a relative error of at most 0.013.
Values may be sent and summed in bfloat16 or wider, within the bound.
A program may use at most 128 MiB of HBM per device.

```python
import math
import jax
import jax.numpy as jnp
import numpy as np
from jax import lax

D = 1024
FF = 1024
TOP = 2
TOK_DEV = 160
EXPERTS = 16
CAP = 40
TOKENS = 5120
N_DP = 4
N_EXPERT = 8


def strengthened(result, key, source, target, blocks, factor):
    owner, partner = [(jnp.arange(result.shape[position]) // (result.shape[position] // blocks)).reshape([-1 if axis == position else 1 for axis in range(result.ndim)]) for position in (source, target)]
    chosen = jax.random.permutation(key, blocks)[partner]
    strong = (owner == chosen) | (owner == (partner + blocks // 2) % blocks)
    return jnp.where(strong, factor * result, result)


def level_of(own_key, dims, split, low, largest):
    gain, own = 1.0, jax.random.fold_in(own_key, 6)
    for dim, blocks in split:
        steps = jnp.exp(jax.random.uniform(jax.random.fold_in(own, dim), (blocks,), jnp.float32, low / len(split), largest / len(split)))
        gain = gain * jnp.repeat(steps, dims[dim] // blocks).reshape([-1 if axis == dim else 1 for axis in range(len(dims))])
    return gain


def deal_out(own_key, own, number, rows, count, top, most, lean):
    sequence = jax.random.permutation(own_key, count)
    crowded, usual = portions_of(count, rows * top, most, lean, True), portions_of(count, rows * top, most, lean, False)
    places = jnp.arange(count)

    def named(sizes, rotation):
        used = int((sizes > 0).sum())
        fixed = max(1, used // 4)
        passed = fixed + (places - fixed + rotation * (used - fixed)) % max(1, count - fixed)
        return jnp.zeros((count,), jnp.int32).at[sequence[jnp.where(places < fixed, places, passed)]].set(jnp.asarray(sizes, jnp.int32))

    sizes = jnp.where(number % 4 == 0, named(crowded, number // 4), named(usual, number - number // 4 - 1))
    mixed = jax.random.permutation(jax.random.fold_in(own, 3), count)
    donor, sink = mixed[0:count // 2 * 2:2], mixed[1:count // 2 * 2:2]
    margin = jnp.minimum(sizes[donor] - 1, most - sizes[sink]) // 2
    margin = jnp.where((donor == sequence[0]) | (sink == sequence[0]) | (sizes[sink] == 0), 0, jnp.maximum(margin, 0))
    passed = jax.random.randint(jax.random.fold_in(own, 4), (count // 2,), 0, 1 << 20) % (margin + 1)
    sizes = sizes.at[donor].add(-passed).at[sink].add(passed)
    items = jnp.searchsorted(jnp.cumsum(sizes), jnp.arange(rows * top), side="right").astype(jnp.int32)
    grid = items.reshape(top, rows).T
    grid = grid[jax.random.permutation(jax.random.fold_in(own, 1), rows)]
    rotation = jax.random.randint(jax.random.fold_in(own, 2), (rows, 1), 0, top)
    return jnp.take_along_axis(grid, (jnp.arange(top)[None, :] + rotation) % top, axis=1)


def portions_of(count, total, bound, lean, full):
    portions = [(1 << 20) // math.isqrt(rank ** lean) + 1 for rank in range(1, count + 1)]
    largest = bound if full else min(bound, max(-(-total // count), total * portions[0] // sum(portions)))
    least = 1 if total - largest >= count - 1 else 0
    given, rest = [largest] + [least] * (count - 1), total - largest - least * (count - 1)
    while rest > 0:
        candidates = [i for i in range(1, count) if given[i] < largest] or [i for i in range(1, count) if given[i] < bound]
        mass, left = sum([portions[i] for i in candidates]), rest
        for i in candidates:
            extra = min(bound - given[i], max(1, left * portions[i] // mass), rest)
            given[i] = given[i] + extra
            rest = rest - extra
    return np.array(given)


def centred(stream_key, extent, spread, most, pieces=(), kind=jnp.bfloat16):
    result = spread * jax.random.normal(stream_key, extent, jnp.float32)
    if pieces:
        result = result * level_of(stream_key, extent, pieces, -0.22, 0.18)
    return jnp.clip(result, -most, most).astype(kind)


def heavy_noise(key, dims, deviation, bound, split, heavy, kind=jnp.bfloat16):
    drawn = deviation * jax.random.normal(key, dims, jnp.float32)
    if split:
        drawn = drawn * level_of(key, dims, split, -0.22, 0.18)
    return jnp.clip(strengthened(drawn, jax.random.fold_in(key, 3), *heavy), -bound, bound).astype(kind)


def setup_inputs(seed: int = 0) -> dict:
    key_list = jax.random.split(jax.random.key(seed), 7)
    tokens = heavy_noise(key_list[0], (TOKENS, D), 1.0, 6.0, ((0, 32),), (0, 1, 32, 2.75))
    expert_ids_keys = jax.random.split(jax.random.fold_in(key_list[1], 1), TOKENS // TOK_DEV)
    expert_ids_turns = jax.random.permutation(jax.random.fold_in(key_list[1], 3), TOKENS // TOK_DEV)
    expert_ids = jax.vmap(lambda own, number: deal_out(jax.random.fold_in(key_list[1], 2), own, number, TOK_DEV, EXPERTS, TOP, CAP, 2))(expert_ids_keys, expert_ids_turns).reshape((TOKENS, TOP))
    router = centred(key_list[2], (D, EXPERTS), (D // 9) ** -0.5, 0.5)
    gate_up_weight = centred(key_list[3], (EXPERTS, D, 2 * FF), D ** -0.5, 0.1875, ((0, 8), (1, 4)))
    down_weight = centred(key_list[4], (EXPERTS, FF, D), FF ** -0.5, 0.1875, ((0, 8), (1, 4)))
    out_grad = centred(key_list[5], (TOKENS, D), 1.0, 6.0, ((0, 32),))
    return dict(tokens=tokens, expert_ids=expert_ids, router=router, gate_up_weight=gate_up_weight, down_weight=down_weight, out_grad=out_grad)


def activate(gate_up, hidden_units):
    gate_part = gate_up[:, :hidden_units]
    up_part = gate_up[:, hidden_units:]
    sigmoid_gate = jax.nn.sigmoid(gate_part)
    active = gate_part * sigmoid_gate
    return (active * up_part).astype(jnp.bfloat16), gate_part, up_part, sigmoid_gate, active


def block_sum(left, right):
    parts = jnp.einsum("gcd,gcf->gdf", left.astype(jnp.float32), right.astype(jnp.float32), precision=lax.Precision.HIGHEST)
    rounded = lax.optimization_barrier(parts.astype(jnp.bfloat16))
    return jnp.sum(rounded.astype(jnp.float32), axis=0)


def reference(tokens, expert_ids, router, gate_up_weight, down_weight, out_grad):
    token_count = tokens.shape[0]
    group_pairs = N_EXPERT * TOK_DEV * TOP
    group_slots = N_EXPERT * CAP
    limit = N_DP * group_slots
    logits = jnp.dot(tokens, router, preferred_element_type=jnp.float32)
    onehot = (expert_ids[:, :, None] == jnp.arange(EXPERTS, dtype=jnp.int32)[None, None, :]).astype(jnp.float32)
    chosen = jnp.sum(logits[:, None, :] * onehot, axis=2)
    gate_first = jax.nn.sigmoid(chosen[:, 0] - chosen[:, 1])
    gate_pair = jnp.stack([gate_first, 1.0 - gate_first], axis=1)
    flat_ids = expert_ids.reshape(-1)
    flat_gates = gate_pair.reshape(-1)
    grouped_ids = flat_ids.reshape(N_DP, group_pairs)

    def find_members(hit_row):
        return jnp.nonzero(hit_row, size=group_slots, fill_value=0)[0].astype(jnp.int32)

    def one_expert(carry, expert):
        mixed_acc, input_acc, gate_acc = carry
        hits = grouped_ids == expert
        local = jax.vmap(find_members)(hits).astype(jnp.int32)
        counts = jnp.sum(hits.astype(jnp.int32), axis=1)
        valid = (jnp.arange(group_slots, dtype=jnp.int32)[None, :] < counts[:, None]).reshape(-1)
        offsets = (jnp.arange(N_DP, dtype=jnp.int32) * group_pairs)[:, None]
        members = (local + offsets).reshape(-1).astype(jnp.int32)
        token_of = (members // TOP).astype(jnp.int32)
        rows_in = tokens[token_of]
        gate_weight_e = gate_up_weight[expert]
        down_weight_e = down_weight[expert]
        gate_up = jnp.dot(rows_in, gate_weight_e, preferred_element_type=jnp.float32)
        hidden, gate_part, up_part, sigmoid_gate, active = activate(gate_up, FF)
        expert_out = jnp.dot(hidden, down_weight_e, preferred_element_type=jnp.float32).astype(jnp.bfloat16)
        gate_of = jnp.where(valid, flat_gates[members], 0.0)
        grad_rows = out_grad[token_of].astype(jnp.float32)
        mixed_acc = mixed_acc.at[token_of].add(gate_of[:, None] * expert_out.astype(jnp.float32))
        inner = jnp.sum(grad_rows * expert_out.astype(jnp.float32), axis=1)
        gate_acc = gate_acc.at[members].add(jnp.where(valid, inner, 0.0))
        slot_grad = (gate_of[:, None] * grad_rows).astype(jnp.bfloat16)
        hidden_grad = jnp.dot(slot_grad, down_weight_e.T, preferred_element_type=jnp.float32)
        gate_grad = hidden_grad * up_part * sigmoid_gate * (1.0 + gate_part * (1.0 - sigmoid_gate))
        up_grad = hidden_grad * active
        pre_grad = jnp.concatenate([gate_grad, up_grad], axis=1).astype(jnp.bfloat16)
        down_part = block_sum(hidden.reshape(N_DP, group_slots, FF), slot_grad.reshape(N_DP, group_slots, D))
        gate_up_part = block_sum(rows_in.reshape(N_DP, group_slots, D), pre_grad.reshape(N_DP, group_slots, 2 * FF))
        input_grad = jnp.dot(pre_grad, gate_weight_e.T, preferred_element_type=jnp.float32).astype(jnp.bfloat16)
        input_acc = input_acc.at[token_of].add(input_grad.astype(jnp.float32))
        return (mixed_acc, input_acc, gate_acc), (gate_up_part, down_part)

    start = (jnp.zeros((token_count, D), jnp.float32), jnp.zeros((token_count, D), jnp.float32), jnp.zeros((token_count * TOP,), jnp.float32))
    (mixed_acc, input_acc, gate_acc), (gate_up_grad, down_grad) = lax.scan(one_expert, start, jnp.arange(EXPERTS, dtype=jnp.int32))
    mixed_out = mixed_acc.astype(jnp.bfloat16)
    gate_grads = gate_acc.reshape(token_count, TOP)
    common = gate_pair[:, 0] * gate_pair[:, 1] * (gate_grads[:, 0] - gate_grads[:, 1])
    logit_grads = common[:, None] * (onehot[:, 0, :] - onehot[:, 1, :])
    tokens_grad = (input_acc + jnp.dot(logit_grads, router.astype(jnp.float32).T, precision=lax.Precision.HIGHEST)).astype(jnp.bfloat16)
    router_grad = jnp.dot(tokens.astype(jnp.float32).T, logit_grads, precision=lax.Precision.HIGHEST)
    return (mixed_out, tokens_grad, router_grad, gate_up_grad, down_grad)
```

```python
import jax
import jax.numpy as jnp
from jax import lax
from jax.sharding import PartitionSpec as P


def activate(gate_up, hidden_units):
    gate_part = gate_up[..., :hidden_units]
    up_part = gate_up[..., hidden_units:]
    sigmoid_gate = jax.nn.sigmoid(gate_part)
    active = gate_part * sigmoid_gate
    return ((active * up_part).astype(jnp.bfloat16), gate_part, up_part, sigmoid_gate, active)


def axis_bits(axis):
    size = lax.axis_size(axis)
    return [1 << position for position in range(size.bit_length() - 1)]


def is_paired(axis):
    size = lax.axis_size(axis)
    return size & (size - 1) == 0


def swap(value, axis, bit):
    return lax.ppermute(value, axis, [(i, i ^ bit) for i in range(lax.axis_size(axis))])


def halves_of(rows):
    if rows % 2:
        return [(0, rows, False)]
    return [(0, rows // 2, False), (rows // 2, rows // 2, True)]


def after(values, *earlier):
    if not earlier:
        return values
    return lax.optimization_barrier((values, earlier))[0]


def own_order(value, axis, rows, dim):
    if not is_paired(axis):
        return value
    me = lax.axis_index(axis)
    return jnp.concatenate(
        [
            lax.dynamic_slice_in_dim(value, (me ^ mask) * rows, rows, axis=dim)
            for mask in range(lax.axis_size(axis))
        ],
        axis=dim,
    )


def gather_rows(block, axis):
    if not is_paired(axis):
        full = lax.all_gather(block, axis, axis=0, tiled=True)
        return full, full[:1]
    bits = axis_bits(axis)
    pieces = {}
    for index, (first, count, turned) in enumerate(halves_of(block.shape[0])):
        held = {0: block[first : first + count]}
        for bit in bits[::-1] if turned else bits:
            held.update({mask | bit: swap(piece, axis, bit) for mask, piece in list(held.items())})
        pieces.update({(mask, index): piece for mask, piece in held.items()})
    full = jnp.concatenate([pieces[place] for place in sorted(pieces)], axis=0)
    return full, [pieces[place] for place in sorted(pieces) if place[0] in bits]


def scatter_rows(part, axis, before_last=(), before_sum=()):
    if not is_paired(axis) or lax.axis_size(axis) == 1:
        return lax.psum_scatter(part, axis, scatter_dimension=0, tiled=True).astype(jnp.float32)
    size = lax.axis_size(axis)
    rows = part.shape[0] // size
    bits = axis_bits(axis)
    done = []
    for first, count, turned in halves_of(rows):
        held = {
            mask: part[mask * rows + first : mask * rows + first + count] for mask in range(size)
        }
        for bit in bits[::-1] if turned else bits:
            if len(held) == 2:
                held = after(held, *before_last)
            came = {mask ^ bit: swap(held[mask], axis, bit) for mask in held if mask & bit}
            if len(held) == 2:
                came = after(came, *before_sum)
            held = {
                mask: held[mask].astype(jnp.float32) + came[mask].astype(jnp.float32)
                for mask in came
            }
            if len(held) > 1:
                held = {mask: total.astype(part.dtype) for mask, total in held.items()}
        done.append(held[0])
    return jnp.concatenate(done, axis=0)


def sum_everywhere(value, axis):
    if not is_paired(axis):
        return lax.psum(value, axis)
    for bit in axis_bits(axis):
        value = value + swap(value, axis, bit)
    return value


def exchange(rows):
    return lax.all_to_all(rows, "expert", split_axis=0, concat_axis=0, tiled=True)


def on_device(tokens, expert_ids, router, gate_up_weight, down_weight, out_grad):
    token_rows, feature_dim = tokens.shape
    pair_count = expert_ids.shape[1]
    owners = lax.axis_size("expert")
    local_count = gate_up_weight.shape[0]
    experts = owners * local_count
    capacity = 2 * pair_count * token_rows // experts
    hidden_units = gate_up_weight.shape[2] // 2
    slot_total = experts * capacity
    onehot = (expert_ids[:, :, None] == jnp.arange(experts, dtype=jnp.int32)[None, None, :]).astype(
        jnp.int32
    )
    per_token = jnp.sum(onehot, axis=1)
    before = jnp.cumsum(per_token, axis=0) - per_token
    position = jnp.sum(before[:, None, :] * onehot, axis=2)
    slot_index = expert_ids * capacity + position
    select = (
        slot_index[:, :, None] == jnp.arange(slot_total, dtype=jnp.int32)[None, None, :]
    ).astype(jnp.bfloat16)
    dispatch = select[:, 0, :] + select[:, 1, :]
    model_rows, unit_rows = gate_up_weight.shape[1], down_weight.shape[1]
    own_tokens = own_order(tokens, "dp", model_rows, 1)
    send_rows = jnp.dot(dispatch.T, own_tokens, preferred_element_type=jnp.float32).astype(jnp.bfloat16)
    weights, gate_up_hop, down_hop = [], [], []
    received = exchange(send_rows.reshape(owners, local_count, capacity, feature_dim))
    for j in range(local_count):
        own_gate_up, own_down = gate_up_weight[j], down_weight[j]
        if j:
            own_gate_up = after(own_gate_up, *gate_up_hop)
            own_down = after(own_down, received, *down_hop)
        full_gate_up, gate_up_hop = gather_rows(own_gate_up, "dp")
        full_down, down_hop = gather_rows(own_down, "dp")
        weights.append((full_gate_up, full_down))
    logits = jnp.dot(tokens, router, preferred_element_type=jnp.float32)
    onehot_float = onehot.astype(jnp.float32)
    chosen = jnp.sum(logits[:, None, :] * onehot_float, axis=2)
    gate_first = jax.nn.sigmoid(chosen[:, 0] - chosen[:, 1])
    gate_pair = jnp.stack([gate_first, 1.0 - gate_first], axis=1)
    grad_float = out_grad.astype(jnp.float32)
    scaled = (gate_pair[:, :, None] * grad_float[:, None, :]).astype(jnp.bfloat16)
    grad_send = jnp.einsum(
        "tks,tkd->sd", select, scaled, preferred_element_type=jnp.float32
    ).astype(jnp.bfloat16)
    grad_recv = exchange(grad_send.reshape(owners, local_count, capacity, feature_dim))

    produced, input_grads, gate_up_parts, down_parts = [], [], [], []
    for j in range(local_count):
        full_gate_up, full_down = weights[j]
        rows_in = received[:, j].reshape(owners * capacity, feature_dim)
        grad_in = grad_recv[:, j].reshape(owners * capacity, feature_dim)
        if j:
            rows_in, grad_in = after((rows_in, grad_in), gate_up_parts[-1], down_parts[-1], input_grads[-1])
        gate_up = jnp.dot(rows_in, full_gate_up, preferred_element_type=jnp.float32)
        hidden, gate_part, up_part, sigmoid_gate, active = activate(gate_up, hidden_units)
        hidden = own_order(hidden, "dp", unit_rows, 1)
        out = jnp.dot(hidden, full_down, preferred_element_type=jnp.float32).astype(jnp.bfloat16)
        produced.append(out.reshape(owners, 1, capacity, feature_dim))
        down_part = lax.dot_general(
            hidden, grad_in, (((0,), (0,)), ((), ())), preferred_element_type=jnp.float32
        ).astype(jnp.bfloat16)
        down_parts.append(down_part)
        hidden_grad = lax.dot_general(
            grad_in, full_down, (((1,), (1,)), ((), ())), preferred_element_type=jnp.float32
        )
        hidden_grad = own_order(hidden_grad, "dp", unit_rows, 1)
        gate_grad = hidden_grad * up_part * sigmoid_gate * (1.0 + gate_part * (1.0 - sigmoid_gate))
        up_grad = hidden_grad * active
        pre_grad = jnp.concatenate([gate_grad, up_grad], axis=1).astype(jnp.bfloat16)
        gate_up_part = lax.dot_general(
            rows_in, pre_grad, (((0,), (0,)), ((), ())), preferred_element_type=jnp.float32
        ).astype(jnp.bfloat16)
        gate_up_parts.append(gate_up_part)
        input_grad = lax.dot_general(
            pre_grad, full_gate_up, (((1,), (1,)), ((), ())), preferred_element_type=jnp.float32
        ).astype(jnp.bfloat16)
        input_grads.append(input_grad.reshape(owners, 1, capacity, feature_dim))
    returned = exchange(jnp.concatenate(produced, axis=1))
    input_back = exchange(jnp.concatenate(input_grads, axis=1))
    expert_out = jnp.einsum(
        "tks,sd->tkd",
        select,
        returned.reshape(slot_total, feature_dim),
        preferred_element_type=jnp.float32,
    )
    mixed_out = jnp.sum(gate_pair[:, :, None] * expert_out, axis=1).astype(jnp.bfloat16)
    gate_grads = jnp.sum(grad_float[:, None, :] * expert_out, axis=2)
    common = gate_pair[:, 0] * gate_pair[:, 1] * (gate_grads[:, 0] - gate_grads[:, 1])
    logit_grads = common[:, None] * (onehot_float[:, 0, :] - onehot_float[:, 1, :])
    router_term = lax.dot_general(
        logit_grads,
        tokens.astype(jnp.float32),
        (((0,), (0,)), ((), ())),
        precision=lax.Precision.HIGHEST,
    )
    router_grad = sum_everywhere(sum_everywhere(router_term, "expert"), "dp").T
    input_pair = jnp.einsum(
        "tks,sd->td",
        select,
        input_back.reshape(slot_total, feature_dim),
        preferred_element_type=jnp.float32,
    )
    input_pair = own_order(input_pair, "dp", model_rows, 1)
    router_float = router.astype(jnp.float32)
    tokens_grad = (
        input_pair + jnp.dot(logit_grads, router_float.T, precision=lax.Precision.HIGHEST)
    ).astype(jnp.bfloat16)
    last = local_count - 1
    down_grads = [
        scatter_rows(part, "dp", (router_term,) if j == last else ())
        for j, part in enumerate(down_parts)
    ]
    gate_up_grads = [
        scatter_rows(
            part,
            "dp",
            (router_term,) if j == last else (),
            (router_grad, tokens_grad) if j == last else (),
        )
        for j, part in enumerate(gate_up_parts)
    ]
    return (
        mixed_out,
        tokens_grad,
        router_grad,
        jnp.stack(gate_up_grads, axis=0),
        jnp.stack(down_grads, axis=0),
    )


def solution(mesh):
    placed = (
        P(("dp", "expert"), None),
        P(("dp", "expert"), None),
        P(),
        P("expert", "dp", None),
        P("expert", "dp", None),
        P(("dp", "expert"), None),
    )
    return jax.shard_map(
        on_device,
        mesh=mesh,
        in_specs=placed,
        out_specs=(
            P(("dp", "expert"), None),
            P(("dp", "expert"), None),
            P(),
            P("expert", "dp", None),
            P("expert", "dp", None),
        ),
        check_vma=False,
    )
```
